256 devices in a mesh: group: 32 (over y, z), inner: 8 (over x, core).
Axes of the slice: x: 4, y: 4, z: 8, core: 2. Of those that a mesh axis runs over, the one named last changes fastest.
Arguments:
- tokens: bfloat16 [4096, 7168], P('group', 'inner'), may hold values from -6 to 6
- routes: int32 [4096, 4], P('group'), may hold values from 0 to 31, all different within a row; in each aligned block of 128 rows (0 to 127, 128 to 255, ...) at most 24 rows name the same one
- gate_weights: float32 [4096, 4], P('group'), may hold values from 0.1 to 1
- w_gate: bfloat16 [32, 7168, 2048], P('group', None, 'inner'), may hold values from -0.0625 to 0.0625
- w_up: bfloat16 [32, 7168, 2048], P('group', None, 'inner'), may hold values from -0.0625 to 0.0625
- w_down: bfloat16 [32, 2048, 7168], P('group', 'inner'), may hold values from -0.125 to 0.125
Outputs:
- moe_out: bfloat16 [4096, 7168], P('group', 'inner')
The draws below stay inside these ranges and needn't reach their ends.
Inputs may be any that keep to these rules, and one draw needn't show every extreme that they name: `routes`: each row names 4 different expert groups. Within each aligned block of 128 rows (the rows of one index of group) no group is named by more than 24 rows, and in some blocks one group is named by exactly 24 rows.
All inputs are finite; a program needn't handle non-finite values.
Results may differ from the reference program's by a relative error of at most 0.014.
Values may be sent and summed in bfloat16 or wider, within the bound.
A program may use at most 128 MiB of HBM per device.

```python
import math
import jax
import jax.numpy as jnp
import numpy as np
from jax import lax

D = 7168
FE = 2048
CHOSEN = 4
TOK_GROUP = 128
CAP = 24
EXPERTS = 32
TOKENS = 4096
N_GROUP = 32
N_INNER = 8


def levels(key, shape, pieces, least, largest):
    gain = 1.0
    for axis_at, blocks in pieces:
        heights = jax.random.uniform(jax.random.fold_in(jax.random.fold_in(key, 6), axis_at), (blocks,), jnp.float32, least / len(pieces), largest / len(pieces))
        gain = gain * jnp.repeat(jnp.exp(heights), shape[axis_at] // blocks).reshape((-1,) + (1,) * (len(shape) - 1 - axis_at))
    return gain


def deal_out(own_key, own, number, rows, count, top, bound, skew):
    ranking = jax.random.permutation(own_key, count)
    crowded, common = shares(count, rows * top, bound, skew, True), shares(count, rows * top, bound, skew, False)
    places = jnp.arange(count)

    def named(tallies, rotation):
        used = int((tallies > 0).sum())
        fixed = max(1, used // 4)
        passed = fixed + (places - fixed + rotation * (used - fixed)) % max(1, count - fixed)
        return jnp.zeros((count,), jnp.int32).at[ranking[jnp.where(places < fixed, places, passed)]].set(jnp.asarray(tallies, jnp.int32))

    tallies = jnp.where(number % 4 == 0, named(crowded, number // 4), named(common, number - number // 4 - 1))
    mixed = jax.random.permutation(jax.random.fold_in(own, 3), count)
    donor, receiver = mixed[0:count // 2 * 2:2], mixed[1:count // 2 * 2:2]
    margin = jnp.minimum(tallies[donor] - 1, bound - tallies[receiver]) // 2
    margin = jnp.where((donor == ranking[0]) | (receiver == ranking[0]) | (tallies[receiver] == 0), 0, jnp.maximum(margin, 0))
    passed = jax.random.randint(jax.random.fold_in(own, 4), (count // 2,), 0, 1 << 20) % (margin + 1)
    tallies = tallies.at[donor].add(-passed).at[receiver].add(passed)
    members = jnp.searchsorted(jnp.cumsum(tallies), jnp.arange(rows * top), side="right").astype(jnp.int32)
    table = members.reshape(top, rows).T
    table = table[jax.random.permutation(jax.random.fold_in(own, 1), rows)]
    rotation = jax.random.randint(jax.random.fold_in(own, 2), (rows, 1), 0, top)
    return jnp.take_along_axis(table, (jnp.arange(top)[None, :] + rotation) % top, axis=1)


def shares(number_of, total, most, lean, full):
    weights = [(1 << 20) // math.isqrt(standing ** lean) + 1 for standing in range(1, number_of + 1)]
    largest = most if full else min(most, max(-(-total // number_of), total * weights[0] // sum(weights)))
    least = 1 if total - largest >= number_of - 1 else 0
    given, rest = [largest] + [least] * (number_of - 1), total - largest - least * (number_of - 1)
    while rest > 0:
        movable = [i for i in range(1, number_of) if given[i] < largest] or [i for i in range(1, number_of) if given[i] < most]
        whole, budget = sum([weights[i] for i in movable]), rest
        for i in movable:
            addition = min(most - given[i], max(1, budget * weights[i] // whole), rest)
            given[i] = given[i] + addition
            rest = rest - addition
    return np.array(given)


def normal_values(key, dims, width, reach, pieces=(), held_as=jnp.bfloat16):
    gain = levels(key, dims, pieces, -0.22, 0.18) if pieces else 1.0
    drawn = jax.random.normal(key, dims, jnp.float32) * width * gain
    return jnp.minimum(jnp.maximum(drawn, -reach), reach).astype(held_as)


def setup_inputs(seed: int = 0) -> dict:
    keys = jax.random.split(jax.random.key(seed), 7)
    tokens = normal_values(keys[0], (TOKENS, D), 1.0, 6.0, ((0, 32), (1, 8)))
    routes_keys = jax.random.split(jax.random.fold_in(keys[1], 1), TOKENS // TOK_GROUP)
    routes_turns = jax.random.permutation(jax.random.fold_in(keys[1], 3), TOKENS // TOK_GROUP)
    routes = jax.vmap(lambda own, number: deal_out(jax.random.fold_in(keys[1], 2), own, number, TOK_GROUP, N_GROUP, CHOSEN, CAP, 2))(routes_keys, routes_turns).reshape((TOKENS, CHOSEN))
    gate_weights = jnp.clip(0.1 + 0.9 * jax.random.uniform(keys[2], (TOKENS, CHOSEN), jnp.float32) ** levels(keys[2], (TOKENS, CHOSEN), ((0, 32),), -0.2, 0.2), 0.1, 1.0)
    w_gate = normal_values(keys[3], (EXPERTS, D, FE), D ** -0.5, 0.0625, ((0, 32), (2, 8)))
    w_up = normal_values(keys[4], (EXPERTS, D, FE), D ** -0.5, 0.0625, ((0, 32), (2, 8)))
    w_down = normal_values(keys[5], (EXPERTS, FE, D), FE ** -0.5, 0.125, ((0, 32), (1, 8)))
    return dict(tokens=tokens, routes=routes, gate_weights=gate_weights, w_gate=w_gate, w_up=w_up, w_down=w_down)


def expert_rows(token_rows, gate_mat, up_mat, down_mat, parts):
    gate_out = jnp.dot(token_rows, gate_mat, preferred_element_type=jnp.float32)
    up_out = jnp.dot(token_rows, up_mat, preferred_element_type=jnp.float32)
    hidden = (jax.nn.silu(gate_out) * up_out).astype(jnp.bfloat16)
    span_size = hidden.shape[1] // parts
    summed = jnp.zeros((token_rows.shape[0], down_mat.shape[1]), jnp.float32)
    for slice_id in range(parts):
        lower = slice_id * span_size
        partial_value = jnp.dot(hidden[:, lower:lower + span_size], down_mat[lower:lower + span_size], preferred_element_type=jnp.float32)
        rounded = lax.optimization_barrier(partial_value.astype(jnp.bfloat16))
        summed = summed + rounded.astype(jnp.float32)
    return summed


def reference(tokens, routes, gate_weights, w_gate, w_up, w_down):
    route_blocks = routes.reshape(N_GROUP, TOK_GROUP, CHOSEN)
    group_ids = jnp.arange(N_GROUP, dtype=jnp.int32)
    onehot = route_blocks[..., None] == group_ids
    chosen = jnp.sum(onehot.astype(jnp.int32), axis=2)
    weight_by = jnp.sum(jnp.where(onehot, gate_weights.reshape(N_GROUP, TOK_GROUP, CHOSEN)[..., None], 0.0), axis=2).astype(jnp.float32)
    slot_of = jnp.cumsum(chosen, axis=1) - 1
    token_blocks = tokens.reshape(N_GROUP, TOK_GROUP, D).astype(jnp.float32)
    slot_ids = jnp.arange(CAP, dtype=jnp.int32)

    def one_expert(totals, expert_id):
        picked = lax.dynamic_index_in_dim(chosen, expert_id, 2, keepdims=False)
        position = lax.dynamic_index_in_dim(slot_of, expert_id, 2, keepdims=False)
        weight_one = lax.dynamic_index_in_dim(weight_by, expert_id, 2, keepdims=False)
        placing = ((picked[:, None, :] == 1) & (position[:, None, :] == slot_ids[None, :, None])).astype(jnp.float32)
        gathered = jnp.einsum("sct,std->scd", placing, token_blocks, precision=lax.Precision.HIGHEST)
        gathered = gathered.astype(jnp.bfloat16).reshape(N_GROUP * CAP, D)
        out_rows = expert_rows(gathered, w_gate[expert_id], w_up[expert_id], w_down[expert_id], N_INNER)
        out_blocks = out_rows.reshape(N_GROUP, CAP, D)
        weight_table = placing * weight_one[:, None, :]
        totals = totals + jnp.einsum("sct,scd->std", weight_table, out_blocks, precision=lax.Precision.HIGHEST)
        return totals, expert_id

    summed, unused_ids = lax.scan(one_expert, jnp.zeros((N_GROUP, TOK_GROUP, D), jnp.float32), jnp.arange(N_GROUP, dtype=jnp.int32))
    return summed.reshape(TOKENS, D).astype(jnp.bfloat16)
```

```python
import jax
import jax.numpy as jnp
from jax import lax
from jax.sharding import PartitionSpec as P


def layout(routes, groups, capacity):
    group_ids = jnp.arange(groups, dtype=jnp.int32)
    onehot = routes[:, :, None] == group_ids[None, None, :]
    chosen = jnp.sum(onehot.astype(jnp.int32), axis=1)
    slot_of = jnp.cumsum(chosen, axis=0) - 1
    slot_ids = jnp.arange(capacity, dtype=jnp.int32)
    placing = (chosen.T[:, None, :] == 1) & (slot_of.T[:, None, :] == slot_ids[None, :, None])
    pick_slot = jnp.take_along_axis(slot_of, routes, axis=1)
    pick_index = routes * capacity + pick_slot
    return (placing, pick_index)


def pack_rows(placing, token_rows):
    packed = jnp.einsum(
        "hct,td->hcd", placing.astype(jnp.bfloat16), token_rows, preferred_element_type=jnp.float32
    )
    return packed.astype(jnp.bfloat16)


def combine(pick_index, gate_weights, returned):
    flat_rows = returned.reshape(returned.shape[0] * returned.shape[1], returned.shape[2])
    taken = jnp.take(flat_rows, pick_index, axis=0).astype(jnp.float32)
    return jnp.sum(taken * gate_weights[:, :, None], axis=1)


def local(tokens, routes, gate_weights, w_gate, w_up, w_down):
    groups = lax.axis_size("group")
    shard_rows = tokens.shape[0]
    capacity = shard_rows * routes.shape[1] * 3 // (2 * groups)
    placing, pick_index = layout(routes, groups, capacity)
    gate_mat = w_gate[0]
    up_mat = w_up[0]
    down_mat = w_down[0]
    arrived = lax.all_to_all(
        pack_rows(placing, tokens), "group", split_axis=0, concat_axis=0, tiled=True
    )
    feature_part = lax.all_gather(arrived, "inner", axis=2, tiled=True)
    gate_add = jnp.einsum("hck,kf->hcf", feature_part, gate_mat, preferred_element_type=jnp.float32)
    up_add = jnp.einsum("hck,kf->hcf", feature_part, up_mat, preferred_element_type=jnp.float32)
    hidden = (jax.nn.silu(gate_add) * up_add).astype(jnp.bfloat16)
    partial_value = jnp.einsum(
        "hcf,fd->hcd", hidden, down_mat, preferred_element_type=jnp.float32
    ).astype(jnp.bfloat16)
    summed = lax.psum_scatter(partial_value, "inner", scatter_dimension=2, tiled=True)
    returned = lax.all_to_all(summed, "group", split_axis=0, concat_axis=0, tiled=True)
    return combine(pick_index, gate_weights, returned).astype(jnp.bfloat16)


def solution(mesh):
    placed = (
        P("group", "inner"),
        P("group", None),
        P("group", None),
        P("group", None, "inner"),
        P("group", None, "inner"),
        P("group", "inner", None),
    )
    return jax.shard_map(
        local, mesh=mesh, in_specs=placed, out_specs=P("group", "inner"), check_vma=False
    )
```
